256 devices in a mesh: seq: 64 (over y, z, core), batch: 4 (over x).
Axes of the slice: x: 4, y: 4, z: 8, core: 2. Of those that a mesh axis runs over, the one named last changes fastest.
Arguments:
- inputs: bfloat16 [4, 16384, 1536], P('batch', 'seq'), may hold values from -6 to 6
- cotangent: bfloat16 [4, 16384, 1536], P('batch', 'seq'), may hold values from -6 to 6
- convolution_kernel: bfloat16 [3, 1536, 384], replicated, may hold values from -0.09375 to 0.09375
- mix_weight: bfloat16 [384, 1536], replicated, may hold values from -0.3125 to 0.3125
Outputs:
- outputs: bfloat16 [4, 16384, 1536], P('batch', 'seq')
- grad_inputs: bfloat16 [4, 16384, 1536], P('batch', 'seq')
- grad_conv: float32 [1769472], P(('seq', 'batch'))
The draws below stay inside these ranges and needn't reach their ends.
All inputs are finite; a program needn't handle non-finite values.
Results may differ from the reference program's by a relative error of at most 0.0054.
Values may be sent and summed in bfloat16 or wider, within the bound.
No kernel may reach another device: no remote copies, remote signals or barrier semaphores. Data moves between devices by JAX's collectives and lax.ppermute only.
A program may use at most 128 MiB of HBM per device.

```python
import math
import jax
import jax.numpy as jnp

C = 1536
H = 384
DILATION_STEP = 16
SEQS = 4
LENGTH = 16384


def block_levels(stream_key, extent, split, low, largest):
    gain = 1.0
    for dim, blocks in split:
        steps = jax.random.uniform(jax.random.fold_in(jax.random.fold_in(stream_key, 6), dim), (blocks,), jnp.float32, low / len(split), largest / len(split))
        gain = gain * jnp.repeat(jnp.exp(steps), extent[dim] // blocks).reshape((-1,) + (1,) * (len(extent) - 1 - dim))
    return gain


def gaussian(stream_key, dims, spread, bound, pieces=(), held_as=jnp.bfloat16):
    gain = block_levels(stream_key, dims, pieces, -0.22, 0.18) if pieces else 1.0
    entries = jax.random.normal(stream_key, dims, jnp.float32) * spread * gain
    return jnp.minimum(jnp.maximum(entries, -bound), bound).astype(held_as)


def setup_inputs(seed: int = 0) -> dict:
    keys = jax.random.split(jax.random.key(seed), 5)
    return {
        "inputs": gaussian(keys[0], (SEQS, LENGTH, C), 1.0, 6.0, ((0, 4), (1, 64))),
        "cotangent": gaussian(keys[1], (SEQS, LENGTH, C), 1.0, 6.0, ((0, 4), (1, 64))),
        "convolution_kernel": gaussian(keys[2], (3, C, H), (3 * C) ** -0.5, 0.09375),
        "mix_weight": gaussian(keys[3], (H, C), H ** -0.5, 0.3125),
    }


def gelu_slope(values):
    return jax.vjp(jax.nn.gelu, values)[1](jnp.ones_like(values))[0]

def shifted_input(make_array, tap_offset):
    sequence_length = make_array.shape[1]
    padded_input = jnp.pad(make_array, ((0, 0), (DILATION_STEP, DILATION_STEP), (0, 0)))
    return padded_input[:, DILATION_STEP + tap_offset:DILATION_STEP + tap_offset + sequence_length]

def to_row_matrix(make_array):
    return make_array.reshape(-1, make_array.shape[-1])

def matrix_multiply(left, right):
    return jnp.dot(left, right, preferred_element_type=jnp.float32)

def reference(inputs, cotangent, convolution_kernel, mix_weight):
    seqs, sequence_length, channels = inputs.shape
    inner = mix_weight.shape[0]
    activated_values = jax.nn.gelu(inputs.astype(jnp.float32)).astype(jnp.bfloat16)
    preactivation = matrix_multiply(to_row_matrix(shifted_input(activated_values, -DILATION_STEP)), convolution_kernel[0])
    preactivation = preactivation + matrix_multiply(to_row_matrix(activated_values), convolution_kernel[1])
    preactivation = preactivation + matrix_multiply(to_row_matrix(shifted_input(activated_values, DILATION_STEP)), convolution_kernel[2])
    hidden = jax.nn.gelu(preactivation).astype(jnp.bfloat16)
    outputs = (to_row_matrix(inputs).astype(jnp.float32) + matrix_multiply(hidden, mix_weight)).astype(jnp.bfloat16)
    grad_hidden = matrix_multiply(to_row_matrix(cotangent), mix_weight.T)
    preactivation_gradient = (grad_hidden * gelu_slope(preactivation)).astype(jnp.bfloat16).reshape(seqs, sequence_length, inner)
    activation_gradient = matrix_multiply(to_row_matrix(shifted_input(preactivation_gradient, DILATION_STEP)), convolution_kernel[0].T)
    activation_gradient = activation_gradient + matrix_multiply(to_row_matrix(preactivation_gradient), convolution_kernel[1].T)
    activation_gradient = activation_gradient + matrix_multiply(to_row_matrix(shifted_input(preactivation_gradient, -DILATION_STEP)), convolution_kernel[2].T)
    float_inputs = to_row_matrix(inputs).astype(jnp.float32)
    grad_inputs = (to_row_matrix(cotangent).astype(jnp.float32) + activation_gradient * gelu_slope(float_inputs)).astype(jnp.bfloat16)
    gradient_rows = to_row_matrix(preactivation_gradient)
    convolution_gradient = jnp.stack([matrix_multiply(to_row_matrix(shifted_input(activated_values, -DILATION_STEP)).T, gradient_rows), matrix_multiply(to_row_matrix(activated_values).T, gradient_rows), matrix_multiply(to_row_matrix(shifted_input(activated_values, DILATION_STEP)).T, gradient_rows)])
    factor = 1.0 / math.sqrt(seqs * sequence_length)
    return (outputs.reshape(seqs, sequence_length, channels), grad_inputs.reshape(seqs, sequence_length, channels), (convolution_gradient * factor).reshape(-1))
```

```python
import math

import jax
import jax.numpy as jnp
from jax import lax
from jax.sharding import PartitionSpec as P

DILATION_STEP = 16
Y, Z, CORES, X = 4, 8, 2, 4
HALF = 40


def seq_pairs(move):
    pairs = []
    for s in range(Y * Z * CORES):
        y, z, c = move(s // (Z * CORES), (s // CORES) % Z, s % CORES)
        pairs.append((s, (y * Z + z) * CORES + c))
    return pairs


def z_turn(z):
    return (z + 2 * (z % 2) - 1) % Z


def z_far(z):
    return (11 - 4 * (((z + 1) // 2) % 2) - z) % Z


def pick(blocks, *indices):
    return jnp.concatenate([lax.dynamic_slice_in_dim(blocks, i, 1, 0) for i in indices], 0)


def sent(values, axis, pairs, dtype=jnp.bfloat16):
    return lax.ppermute(values.astype(dtype), axis, pairs).astype(jnp.float32)


def neighbours(edge_tail, edge_head):
    count = lax.axis_size("seq")
    before = lax.ppermute(edge_tail, "seq", [(i, i + 1) for i in range(count - 1)])
    after = lax.ppermute(edge_head, "seq", [(i + 1, i) for i in range(count - 1)])
    return before, after


def gelu_slope(values):
    return jax.vjp(jax.nn.gelu, values)[1](jnp.ones_like(values))[0]


def y_rounds(blocks, y, first, second):
    one = seq_pairs(lambda y, z, c: (y ^ first, z, c))
    two = seq_pairs(lambda y, z, c: (y ^ second, z, c))
    kept = pick(blocks, y, y ^ second) + sent(
        pick(blocks, y ^ first, y ^ first ^ second), "seq", one
    )
    return kept[0] + sent(kept[1], "seq", two)


def owner_sum(gradient):
    s = lax.axis_index("seq")
    x = lax.axis_index("batch")
    y, z, c = s // (Z * CORES), (s // CORES) % Z, s % CORES
    rows = gradient.shape[0] // (Y * Z * CORES)
    cols = gradient.shape[1]
    blocks = gradient.reshape(Y * Z, CORES, rows, cols)
    other = lax.dynamic_index_in_dim(blocks, 1 - c, 1, keepdims=False)
    mine = lax.dynamic_index_in_dim(blocks, c, 1, keepdims=False)
    mine = mine + sent(other, "seq", seq_pairs(lambda y, z, c: (y, z, 1 - c)))
    mine = mine.reshape(Y, Z, rows, cols)
    part = jnp.concatenate(
        [y_rounds(mine[:, :, :HALF], y, 1, 3), y_rounds(mine[:, :, HALF:], y, 3, 1)], 1
    )
    near = z ^ 1
    part = pick(part, z, z_far(z), z_turn(z), z_far(z_turn(z))) + sent(
        pick(part, near, z_far(near), z_turn(near), z_far(z_turn(near))),
        "seq",
        seq_pairs(lambda y, z, c: (y, z ^ 1, c)),
    )
    part = part[:2] + sent(part[2:], "seq", seq_pairs(lambda y, z, c: (y, z_turn(z), c)))
    part = part[0] + sent(
        part[1], "seq", seq_pairs(lambda y, z, c: (y, z_far(z), c)), jnp.float32
    )
    part = part.reshape(X, rows // X, cols)
    part = pick(part, x, x ^ 3) + sent(
        pick(part, x ^ 1, x ^ 2), "batch", [(i, i ^ 1) for i in range(X)], jnp.float32
    )
    part = part[0] + sent(part[1], "batch", [(i, i ^ 3) for i in range(X)], jnp.float32)
    return part.reshape(-1)


def body(inputs, cotangent, convolution_kernel, mix_weight):
    seqs, position_count, channels = inputs.shape
    x = inputs[0]
    ct = cotangent[0]
    inner = mix_weight.shape[0]
    step = DILATION_STEP
    before, after = neighbours(x[-step:], x[:step])
    padded = jnp.concatenate([before, x, after], 0)
    activated = jax.nn.gelu(padded.astype(jnp.float32)).astype(jnp.bfloat16)
    taps = jnp.concatenate(
        [activated[k * step : k * step + position_count] for k in range(3)], 1
    )
    kernel_rows = convolution_kernel.reshape(3 * channels, inner)
    preact = jnp.dot(taps, kernel_rows, preferred_element_type=jnp.float32)
    grad_hidden = lax.dot_general(
        ct, mix_weight, (((1,), (1,)), ((), ())), preferred_element_type=jnp.float32
    )
    pre_grad = (grad_hidden * gelu_slope(preact)).astype(jnp.bfloat16)
    gradient = lax.dot_general(
        taps, pre_grad, (((0,), (0,)), ((), ())), preferred_element_type=jnp.float32
    )
    mine = owner_sum(gradient)
    factor = 1.0 / math.sqrt(seqs * position_count * lax.axis_size("seq") * lax.axis_size("batch"))
    grad_conv = mine * factor

    before, after = neighbours(pre_grad[-step:], pre_grad[:step])
    padded_grad = jnp.concatenate([before, pre_grad, after], 0)
    hidden = jax.nn.gelu(preact).astype(jnp.bfloat16)
    mixed = jnp.dot(hidden, mix_weight, preferred_element_type=jnp.float32)
    outputs = (x.astype(jnp.float32) + mixed).astype(jnp.bfloat16)
    act_grad = sum(
        lax.dot_general(
            padded_grad[(2 - k) * step : (2 - k) * step + position_count],
            convolution_kernel[k],
            (((1,), (1,)), ((), ())),
            preferred_element_type=jnp.float32,
        )
        for k in range(3)
    )
    grad_inputs = (
        ct.astype(jnp.float32) + act_grad * gelu_slope(x.astype(jnp.float32))
    ).astype(jnp.bfloat16)
    return outputs[None], grad_inputs[None], grad_conv


def solution(mesh):
    in_specs = (P("batch", "seq", None), P("batch", "seq", None), P(), P())
    out_specs = (P("batch", "seq", None), P("batch", "seq", None), P(("seq", "batch")))
    return jax.shard_map(body, mesh=mesh, in_specs=in_specs, out_specs=out_specs, check_vma=False)
```

```python
import math

import jax
import jax.numpy as jnp
from jax import lax
from jax.experimental import pallas as pl
from jax.experimental.pallas import tpu as pltpu
from jax.sharding import Mesh, PartitionSpec as P

DILATION_STEP = 16
Y, Z, CORES, X = 4, 8, 2, 4
SEQ = ("y", "z", "core")


def neighbours(tail, head):
    count = Y * Z * CORES
    before = lax.ppermute(tail, SEQ, [(i, i + 1) for i in range(count - 1)])
    after = lax.ppermute(head, SEQ, [(i + 1, i) for i in range(count - 1)])
    return before, after


def swap_cores(values):
    return lax.ppermute(values, "core", [(0, 1), (1, 0)])


def gelu(values):
    return jax.nn.gelu(values.astype(jnp.float32)).astype(jnp.bfloat16)


def gelu_slope(values):
    return jax.vjp(jax.nn.gelu, values)[1](jnp.ones_like(values))[0]


def shifted(padded, count):
    return jnp.concatenate(
        [padded[k * DILATION_STEP : k * DILATION_STEP + count] for k in range(3)], 1
    )


def owned_rows(rows, core):
    shape = (X * Z * rows, Z * CORES * X * rows)
    target = lax.broadcasted_iota(jnp.int32, shape, 0)
    source = lax.broadcasted_iota(jnp.int32, shape, 1)
    x, z, i = target // (Z * rows), (target // rows) % Z, target % rows
    return (source == ((z * CORES + core) * X + x) * rows + i).astype(jnp.bfloat16)


def gradient_kernel(act_a, act_b, grad_a, grad_b, select, out):
    count, inner = grad_a.shape
    channels = act_a.shape[1]
    chunk = 384
    per_y = 3 * channels // Y // chunk
    left_a, left_b = grad_a[...].T, grad_b[...].T
    for y in range(Y):
        parts = []
        for j in range(y * per_y, (y + 1) * per_y):
            tap, ch = divmod(j * chunk, channels)
            rows = slice(tap * DILATION_STEP, tap * DILATION_STEP + count)
            part = jnp.dot(
                left_a, act_a[rows, ch : ch + chunk], preferred_element_type=jnp.float32
            ) + jnp.dot(left_b, act_b[rows, ch : ch + chunk], preferred_element_type=jnp.float32)
            parts.append(part.astype(jnp.bfloat16))
        block = lax.dot_general(
            select[...],
            jnp.concatenate(parts, 1),
            (((1,), (1,)), ((), ())),
            preferred_element_type=jnp.float32,
        ).astype(jnp.bfloat16)
        for x in range(X):
            size = block.shape[0] // X
            out[y * X + x] = block[x * size : (x + 1) * size]


def owner_sum(act_a, act_b, grad_a, grad_b):
    inner = grad_a.shape[1]
    rows = 3 * act_a.shape[1] // (Y * Z * CORES * X)
    select = owned_rows(rows, lax.axis_index("core"))
    ordered = pl.pallas_call(
        gradient_kernel,
        out_shape=jax.ShapeDtypeStruct((Y * X, Z * rows, inner), jnp.bfloat16),
        in_specs=[pl.BlockSpec(memory_space=pltpu.VMEM)] * 5,
        out_specs=pl.BlockSpec(memory_space=pltpu.VMEM),
        compiler_params=pltpu.CompilerParams(vmem_limit_bytes=24 << 20),
        cost_estimate=pl.CostEstimate(
            flops=4 * 10**9, bytes_accessed=6 * 10**6, transcendentals=0
        ),
    )(act_a, act_b, grad_a, grad_b, select)
    terms = lax.all_to_all(ordered, ("y", "x"), 0, 0, tiled=True)
    part = jnp.sum(terms.astype(jnp.float32), 0).astype(jnp.bfloat16)
    terms = lax.all_to_all(part.reshape(Z, rows, inner), "z", 0, 0, tiled=True)
    return jnp.sum(terms.astype(jnp.float32), 0).reshape(-1)


def body(inputs, cotangent, convolution_kernel, mix_weight):
    seqs, position_count, channels = inputs.shape
    x = inputs[0]
    ct = cotangent[0]
    inner = mix_weight.shape[0]
    step = DILATION_STEP
    before, after = neighbours(x[-step:], x[:step])
    activated = jnp.concatenate([gelu(before), gelu(x), gelu(after)], 0)
    activated_pair = swap_cores(activated)
    taps = shifted(activated, position_count)
    kernel_rows = convolution_kernel.reshape(3 * channels, inner)
    preact = jnp.dot(taps, kernel_rows, preferred_element_type=jnp.float32)
    grad_hidden = lax.dot_general(
        ct, mix_weight, (((1,), (1,)), ((), ())), preferred_element_type=jnp.float32
    )
    pre_grad = (grad_hidden * gelu_slope(preact)).astype(jnp.bfloat16)
    pre_grad_pair = swap_cores(pre_grad)
    mine = owner_sum(activated, activated_pair, pre_grad, pre_grad_pair)
    factor = 1.0 / math.sqrt(seqs * position_count * Y * Z * CORES * X)
    grad_conv = mine * factor

    before, after = neighbours(pre_grad[-step:], pre_grad[:step])
    padded_grad = jnp.concatenate([before, pre_grad, after], 0)
    hidden = gelu(preact)
    mixed = jnp.dot(hidden, mix_weight, preferred_element_type=jnp.float32)
    outputs = (x.astype(jnp.float32) + mixed).astype(jnp.bfloat16)
    act_grad = sum(
        lax.dot_general(
            padded_grad[(2 - k) * step : (2 - k) * step + position_count],
            convolution_kernel[k],
            (((1,), (1,)), ((), ())),
            preferred_element_type=jnp.float32,
        )
        for k in range(3)
    )
    grad_inputs = (
        ct.astype(jnp.float32) + act_grad * gelu_slope(x.astype(jnp.float32))
    ).astype(jnp.bfloat16)
    return outputs[None], grad_inputs[None], grad_conv


def solution(mesh):
    devices = mesh.devices.reshape(Y, Z, CORES, X)
    fine = Mesh(devices, ("y", "z", "core", "x"))
    rows = P("x", SEQ, None)
    return jax.shard_map(
        body,
        mesh=fine,
        in_specs=(rows, rows, P(), P()),
        out_specs=(rows, rows, P(("y", "z", "core", "x"))),
        check_vma=False,
    )
```

```python
import math

import jax
import jax.numpy as jnp
import numpy as np
from jax import lax
from jax.experimental import pallas as pl
from jax.experimental.pallas import tpu as pltpu
from jax.sharding import Mesh, PartitionSpec as P

DILATION_STEP = 16
Y, Z, CORES, X = 4, 8, 2, 4
SEQ = ("y", "z", "core")


def next_chip_edges(edge):
    pairs = [(2 * k + 1, 2 * k + 2) for k in range(Y * Z - 1)]
    return lax.ppermute(edge, SEQ, pairs + [(b, a) for a, b in pairs])


def swap_cores(values):
    return lax.ppermute(values, "core", [(0, 1), (1, 0)])


def gelu(values):
    return jax.nn.gelu(values.astype(jnp.float32)).astype(jnp.bfloat16)


def gelu_slope(values):
    return jax.vjp(jax.nn.gelu, values)[1](jnp.ones_like(values))[0]


def shifted(padded, count):
    return jnp.concatenate(
        [padded[k * DILATION_STEP : k * DILATION_STEP + count] for k in range(3)], 1
    )


def owned_rows(rows):
    piece = 2 * rows + 4
    held = np.zeros((CORES, Z // 2, X * piece, 384), np.float32)
    for core in range(CORES):
        for z in range(Z):
            q = z // 2
            for x in range(X):
                for i in range(rows):
                    target = x * piece + 4 * (q % 2) + (z % 2) * rows + i
                    held[core, q, target, ((z * CORES + core) * X + x) * rows + i - 256 * q] = 1
    return held.astype(jnp.bfloat16)


def gradient_kernel(
    core, act_a, act_b, grad_a, grad_b, select_all, ordered, whole, select, sem
):
    fetch = pltpu.make_async_copy(select_all.at[core[0]], select, sem)
    fetch.start()
    count, inner = grad_a.shape
    channels = act_a.shape[1]
    left_a, left_b = grad_a[...].T, grad_b[...].T
    width = 512
    for j in range(3 * channels // width):
        tap, ch = divmod(j * width, channels)
        rows = slice(tap * DILATION_STEP, tap * DILATION_STEP + count)
        part = jnp.dot(
            left_a, act_a[rows, ch : ch + width], preferred_element_type=jnp.float32
        ) + jnp.dot(left_b, act_b[rows, ch : ch + width], preferred_element_type=jnp.float32)
        whole[:, j * width : (j + 1) * width] = part.astype(jnp.bfloat16)
    fetch.wait()
    pairs, piece, window = select.shape[0], select.shape[1] // X, select.shape[2]
    block = 3 * channels // Y
    for y in range(Y):
        blocks = []
        for q in range(pairs):
            start = y * block + q * 256
            blocks.append(
                lax.dot_general(
                    select[q],
                    whole[:, start : start + window],
                    (((1,), (1,)), ((), ())),
                    preferred_element_type=jnp.float32,
                )
            )
        for x in range(X):
            a, b, c, d = (held[x * piece : (x + 1) * piece] for held in blocks)
            ordered[y * X + x] = jnp.concatenate(
                [a[:32], a[32:] + b[:8], b[8:], c[:32], c[32:] + d[:8], d[8:]], 0
            ).astype(jnp.bfloat16)


def y_x_terms(act_a, act_b, grad_a, grad_b):
    inner = grad_a.shape[1]
    rows = 3 * act_a.shape[1] // (Y * Z * CORES * X)
    select = jnp.asarray(owned_rows(rows))
    vmem = pl.BlockSpec(memory_space=pltpu.VMEM)
    ordered = pl.pallas_call(
        gradient_kernel,
        out_shape=jax.ShapeDtypeStruct((Y * X, Z * rows, inner), jnp.bfloat16),
        in_specs=[pl.BlockSpec(memory_space=pltpu.SMEM)]
        + [vmem] * 4
        + [pl.BlockSpec(memory_space=pl.ANY)],
        out_specs=vmem,
        scratch_shapes=[
            pltpu.VMEM((inner, 3 * act_a.shape[1]), jnp.bfloat16),
            pltpu.VMEM(select.shape[1:], jnp.bfloat16),
            pltpu.SemaphoreType.DMA,
        ],
        compiler_params=pltpu.CompilerParams(vmem_limit_bytes=24 << 20),
        cost_estimate=pl.CostEstimate(
            flops=3 * 10**9, bytes_accessed=6 * 10**6, transcendentals=0
        ),
    )(lax.axis_index("core").astype(jnp.int32)[None], act_a, act_b, grad_a, grad_b, select)
    return lax.all_to_all(ordered, ("y", "x"), 0, 0, tiled=True)


def z_sum(terms):
    rows, inner = terms.shape[1] // Z, terms.shape[2]
    part = jnp.sum(terms.astype(jnp.float32), 0).astype(jnp.bfloat16)
    terms = lax.all_to_all(part.reshape(Z, rows, inner), "z", 0, 0, tiled=True)
    return jnp.sum(terms.astype(jnp.float32), 0).reshape(-1)


def body(inputs, cotangent, convolution_kernel, mix_weight):
    seqs, position_count, channels = inputs.shape
    x = inputs[0]
    ct = cotangent[0]
    inner = mix_weight.shape[0]
    step = DILATION_STEP
    core = lax.axis_index("core")
    last = position_count - step

    def padded(values, outer, inner):
        first = core == 0
        return jnp.concatenate(
            [jnp.where(first, outer, inner), values, jnp.where(first, inner, outer)], 0
        )

    outer = next_chip_edges(lax.dynamic_slice_in_dim(x, core * last, step, 0))
    inside = swap_cores(lax.dynamic_slice_in_dim(x, (1 - core) * last, step, 0))
    activated = padded(gelu(x), gelu(outer), gelu(inside))
    activated = lax.optimization_barrier(activated)
    activated_pair = swap_cores(activated)
    taps = shifted(activated, position_count)
    kernel_rows = convolution_kernel.reshape(3 * channels, inner)
    preact = jnp.dot(taps, kernel_rows, preferred_element_type=jnp.float32)
    preact, activated_pair = lax.optimization_barrier((preact, activated_pair))
    grad_hidden = lax.dot_general(
        ct, mix_weight, (((1,), (1,)), ((), ())), preferred_element_type=jnp.float32
    )
    pre_grad = (grad_hidden * gelu_slope(preact)).astype(jnp.bfloat16)
    pre_grad_pair = swap_cores(pre_grad)
    terms = y_x_terms(activated, activated_pair, pre_grad, pre_grad_pair)

    outer = next_chip_edges(lax.dynamic_slice_in_dim(pre_grad, core * last, step, 0))
    inside = lax.dynamic_slice_in_dim(pre_grad_pair, core * last, step, 0)
    padded_grad = padded(pre_grad, outer, inside)
    hidden = gelu(preact)
    mixed = jnp.dot(hidden, mix_weight, preferred_element_type=jnp.float32)
    outputs = (x.astype(jnp.float32) + mixed).astype(jnp.bfloat16)
    act_grad = sum(
        lax.dot_general(
            padded_grad[(2 - k) * step : (2 - k) * step + position_count],
            convolution_kernel[k],
            (((1,), (1,)), ((), ())),
            preferred_element_type=jnp.float32,
        )
        for k in range(3)
    )
    grad_inputs = (
        ct.astype(jnp.float32) + act_grad * gelu_slope(x.astype(jnp.float32))
    ).astype(jnp.bfloat16)
    terms, grad_inputs = lax.optimization_barrier((terms, grad_inputs))
    factor = 1.0 / math.sqrt(seqs * position_count * Y * Z * CORES * X)
    grad_conv = z_sum(terms) * factor
    return outputs[None], grad_inputs[None], grad_conv


def solution(mesh):
    devices = mesh.devices.reshape(Y, Z, CORES, X)
    fine = Mesh(devices, ("y", "z", "core", "x"))
    rows = P("x", SEQ, None)
    return jax.shard_map(
        body,
        mesh=fine,
        in_specs=(rows, rows, P(), P()),
        out_specs=(rows, rows, P(("y", "z", "core", "x"))),
        check_vma=False,
    )
```

```python
import math

import jax
import jax.numpy as jnp
import numpy as np
from jax import lax
from jax.experimental import pallas as pl
from jax.experimental.pallas import tpu as pltpu
from jax.sharding import Mesh, PartitionSpec as P

DILATION_STEP = 16
Y, Z, CORES, X = 4, 8, 2, 4
SEQ = ("y", "z", "core")


def next_chip_edges(edge):
    pairs = [(2 * k + 1, 2 * k + 2) for k in range(Y * Z - 1)]
    return lax.ppermute(edge, SEQ, pairs + [(b, a) for a, b in pairs])


def swap_cores(values):
    return lax.ppermute(values, "core", [(0, 1), (1, 0)])


def gelu(values):
    return jax.nn.gelu(values.astype(jnp.float32)).astype(jnp.bfloat16)


def gelu_slope(values):
    return jax.vjp(jax.nn.gelu, values)[1](jnp.ones_like(values))[0]


def owned_rows(rows):
    piece = rows + 6
    held = np.zeros((CORES, Z, X * piece, 256), np.float32)
    for core in range(CORES):
        for z in range(Z):
            for x in range(X):
                for i in range(rows):
                    target = x * piece + rows * z % 8 + i
                    held[core, z, target, ((z * CORES + core) * X + x) * rows + i - 128 * z] = 1
    return held.astype(jnp.bfloat16)


def slope(values):
    root, cube = 0.7978845608, 0.044715
    square = values * values
    wave = jnp.tanh(root * values * (1.0 + cube * square))
    return 0.5 * (1.0 + wave) + 0.5 * values * (1.0 - wave * wave) * (
        root * (1.0 + 3.0 * cube * square)
    )


def gelu_kernel(x_far, ct_far, kernel_far, mix_far, act, ct, kernel, mix, x, sems):
    copies = [
        pltpu.make_async_copy(source, target, sems.at[i])
        for i, (source, target) in enumerate(
            ((x_far, x), (kernel_far, kernel), (mix_far, mix), (ct_far, ct))
        )
    ]
    for copy in copies:
        copy.start()
    copies[0].wait()
    act[...] = gelu(x[...])
    for copy in copies[1:]:
        copy.wait()


def gelu_and_fetch(x, ct, kernel, mix):
    vmem = pl.BlockSpec(memory_space=pltpu.VMEM)
    return pl.pallas_call(
        gelu_kernel,
        out_shape=tuple(pltpu.VMEM(a.shape, jnp.bfloat16) for a in (x, ct, kernel, mix)),
        in_specs=[pl.BlockSpec(memory_space=pl.ANY)] * 4,
        out_specs=(vmem,) * 4,
        scratch_shapes=[pltpu.VMEM(x.shape, jnp.bfloat16), pltpu.SemaphoreType.DMA((4,))],
        compiler_params=pltpu.CompilerParams(vmem_limit_bytes=24 << 20),
        cost_estimate=pl.CostEstimate(
            flops=4 * 10**6, bytes_accessed=7 * 10**6, transcendentals=4 * 10**5
        ),
    )(*(pltpu.with_memory_space_constraint(a, pltpu.HBM) for a in (x, ct, kernel, mix)))


def pre_grad_kernel(act, ct, kernel, mix, preact, pre_grad):
    count = ct.shape[0]
    total = sum(
        jnp.dot(
            act[tap * DILATION_STEP : tap * DILATION_STEP + count],
            kernel[tap],
            preferred_element_type=jnp.float32,
        )
        for tap in range(3)
    )
    preact[...] = total
    grad_hidden = lax.dot_general(
        ct[...], mix[...], (((1,), (1,)), ((), ())), preferred_element_type=jnp.float32
    )
    pre_grad[...] = (grad_hidden * slope(preact[...])).astype(jnp.bfloat16)


def preact_and_grad(act, ct, kernel, mix):
    count, inner = ct.shape[0], mix.shape[0]
    vmem = pl.BlockSpec(memory_space=pltpu.VMEM)
    return pl.pallas_call(
        pre_grad_kernel,
        out_shape=(
            jax.ShapeDtypeStruct((count, inner), jnp.float32),
            jax.ShapeDtypeStruct((count, inner), jnp.bfloat16),
        ),
        in_specs=[vmem] * 4,
        out_specs=(vmem, vmem),
        compiler_params=pltpu.CompilerParams(vmem_limit_bytes=24 << 20),
        cost_estimate=pl.CostEstimate(
            flops=12 * 10**8, bytes_accessed=6 * 10**6, transcendentals=10**5
        ),
    )(act, ct, kernel, mix)


def gradient_kernel(
    core, act_a, act_b, grad_a, grad_b, select_all, ordered_far,
    whole, select, ordered, sem, out_sems,
):
    fetch = pltpu.make_async_copy(select_all.at[core[0]], select, sem)
    fetch.start()
    count, inner = grad_a.shape
    channels = act_a.shape[1]
    left_a, left_b = grad_a[...].T, grad_b[...].T
    width = 512
    for j in range(3 * channels // width):
        tap, ch = divmod(j * width, channels)
        rows = slice(tap * DILATION_STEP, tap * DILATION_STEP + count)
        part = jnp.dot(
            left_a, act_a[rows, ch : ch + width], preferred_element_type=jnp.float32
        ) + jnp.dot(left_b, act_b[rows, ch : ch + width], preferred_element_type=jnp.float32)
        whole[:, j * width : (j + 1) * width] = part.astype(jnp.bfloat16)
    fetch.wait()
    piece, window = select.shape[1] // X, select.shape[2]
    block = 3 * channels // Y
    stores = []
    for y in range(Y):
        blocks = []
        for z in range(Z):
            start = y * block + z * 128
            blocks.append(
                lax.dot_general(
                    select[z],
                    whole[:, start : start + window],
                    (((1,), (1,)), ((), ())),
                    preferred_element_type=jnp.float32,
                )
            )
        for x in range(X):
            parts = []
            for four in range(0, Z, 4):
                a, b, c, d = (
                    held[x * piece : (x + 1) * piece] for held in blocks[four : four + 4]
                )
                parts += [a[:16], a[16:] + b[:8], b[8:16], b[16:] + c[:8]]
                parts += [c[8:16], c[16:] + d[:8], d[8:]]
            ordered[y * X + x] = jnp.concatenate(parts, 0).astype(jnp.bfloat16)
        span = slice(y * X, (y + 1) * X)
        stores.append(pltpu.make_async_copy(ordered.at[span], ordered_far.at[span], out_sems.at[y]))
        stores[-1].start()
    for store in stores:
        store.wait()


def y_x_terms(act_a, act_b, grad_a, grad_b):
    inner = grad_a.shape[1]
    rows = 3 * act_a.shape[1] // (Y * Z * CORES * X)
    select = jnp.asarray(owned_rows(rows))
    vmem = pl.BlockSpec(memory_space=pltpu.VMEM)
    ordered = pl.pallas_call(
        gradient_kernel,
        out_shape=pltpu.HBM((Y * X, Z * rows, inner), jnp.bfloat16),
        in_specs=[pl.BlockSpec(memory_space=pltpu.SMEM)]
        + [vmem] * 4
        + [pl.BlockSpec(memory_space=pl.ANY)],
        out_specs=pl.BlockSpec(memory_space=pl.ANY),
        scratch_shapes=[
            pltpu.VMEM((inner, 3 * act_a.shape[1]), jnp.bfloat16),
            pltpu.VMEM(select.shape[1:], jnp.bfloat16),
            pltpu.VMEM((Y * X, Z * rows, inner), jnp.bfloat16),
            pltpu.SemaphoreType.DMA,
            pltpu.SemaphoreType.DMA((Y,)),
        ],
        compiler_params=pltpu.CompilerParams(vmem_limit_bytes=24 << 20),
        cost_estimate=pl.CostEstimate(
            flops=3 * 10**9, bytes_accessed=6 * 10**6, transcendentals=0
        ),
    )(lax.axis_index("core").astype(jnp.int32)[None], act_a, act_b, grad_a, grad_b, pltpu.with_memory_space_constraint(select, pltpu.HBM))
    return lax.all_to_all(ordered, ("y", "x"), 0, 0, tiled=True)


def z_sum(terms):
    rows, inner = terms.shape[1] // Z, terms.shape[2]
    part = jnp.sum(terms.astype(jnp.float32), 0).astype(jnp.bfloat16)
    terms = lax.all_to_all(part.reshape(Z, rows, inner), "z", 0, 0, tiled=True)
    return jnp.sum(terms.astype(jnp.float32), 0).reshape(-1)


def body(inputs, cotangent, convolution_kernel, mix_weight):
    seqs, position_count, channels = inputs.shape
    x = inputs[0]
    ct = cotangent[0]
    step = DILATION_STEP
    core = lax.axis_index("core")
    last = position_count - step

    def padded(values, outer, inner):
        first = core == 0
        return jnp.concatenate(
            [jnp.where(first, outer, inner), values, jnp.where(first, inner, outer)], 0
        )

    outer = next_chip_edges(lax.dynamic_slice_in_dim(x, core * last, step, 0))
    inside = swap_cores(lax.dynamic_slice_in_dim(x, (1 - core) * last, step, 0))
    act, ct_near, kernel_near, mix_near = gelu_and_fetch(x, ct, convolution_kernel, mix_weight)
    activated = padded(act, gelu(outer), gelu(inside))
    activated = lax.optimization_barrier(activated)
    activated_pair = swap_cores(activated)
    preact, pre_grad = preact_and_grad(activated, ct_near, kernel_near, mix_near)
    pre_grad, activated_pair = lax.optimization_barrier((pre_grad, activated_pair))
    pre_grad_pair = swap_cores(pre_grad)
    terms = y_x_terms(activated, activated_pair, pre_grad, pre_grad_pair)

    outer = next_chip_edges(lax.dynamic_slice_in_dim(pre_grad, core * last, step, 0))
    inside = lax.dynamic_slice_in_dim(pre_grad_pair, core * last, step, 0)
    padded_grad = padded(pre_grad, outer, inside)
    hidden = gelu(preact)
    mixed = jnp.dot(hidden, mix_weight, preferred_element_type=jnp.float32)
    outputs = (x.astype(jnp.float32) + mixed).astype(jnp.bfloat16)
    act_grad = sum(
        lax.dot_general(
            padded_grad[(2 - k) * step : (2 - k) * step + position_count],
            convolution_kernel[k],
            (((1,), (1,)), ((), ())),
            preferred_element_type=jnp.float32,
        )
        for k in range(3)
    )
    grad_inputs = (
        ct.astype(jnp.float32) + act_grad * gelu_slope(x.astype(jnp.float32))
    ).astype(jnp.bfloat16)
    terms, grad_inputs = lax.optimization_barrier((terms, grad_inputs))
    factor = 1.0 / math.sqrt(seqs * position_count * Y * Z * CORES * X)
    grad_conv = z_sum(terms) * factor
    return outputs[None], grad_inputs[None], grad_conv


def solution(mesh):
    devices = mesh.devices.reshape(Y, Z, CORES, X)
    fine = Mesh(devices, ("y", "z", "core", "x"))
    rows = P("x", SEQ, None)
    return jax.shard_map(
        body,
        mesh=fine,
        in_specs=(rows, rows, P(), P()),
        out_specs=(rows, rows, P(("y", "z", "core", "x"))),
        check_vma=False,
    )
```

```python
import math

import jax
import jax.numpy as jnp
import numpy as np
from jax import lax
from jax.experimental import pallas as pl
from jax.experimental.pallas import tpu as pltpu
from jax.sharding import Mesh, PartitionSpec as P

DILATION_STEP = 16
Y, Z, CORES, X = 4, 8, 2, 4
SEQ = ("y", "z", "core")


def next_chip_edges(edge):
    pairs = [(2 * k + 1, 2 * k + 2) for k in range(Y * Z - 1)]
    return lax.ppermute(edge, SEQ, pairs + [(b, a) for a, b in pairs])


def swap_cores(values):
    return lax.ppermute(values, "core", [(0, 1), (1, 0)])


def gelu(values):
    return jax.nn.gelu(values.astype(jnp.float32)).astype(jnp.bfloat16)


def gelu_slope(values):
    return jax.vjp(jax.nn.gelu, values)[1](jnp.ones_like(values))[0]


def owned_rows(rows):
    piece = rows + 6
    held = np.zeros((CORES, Z, X * piece, 256), np.float32)
    for core in range(CORES):
        for z in range(Z):
            for x in range(X):
                for i in range(rows):
                    target = x * piece + rows * z % 8 + i
                    held[core, z, target, ((z * CORES + core) * X + x) * rows + i - 128 * z] = 1
    return held.astype(jnp.bfloat16)


def slope(values):
    root, cube = 0.7978845608, 0.044715
    square = values * values
    wave = jnp.tanh(root * values * (1.0 + cube * square))
    return 0.5 * (1.0 + wave) + 0.5 * values * (1.0 - wave * wave) * (
        root * (1.0 + 3.0 * cube * square)
    )


def gelu_kernel(x_far, ct_far, kernel_far, mix_far, act, ct, kernel, mix, x, sems):
    copies = [
        pltpu.make_async_copy(source, target, sems.at[i])
        for i, (source, target) in enumerate(
            ((x_far, x), (kernel_far, kernel), (mix_far, mix), (ct_far, ct))
        )
    ]
    for copy in copies:
        copy.start()
    copies[0].wait()
    act[...] = gelu(x[...])
    for copy in copies[1:]:
        copy.wait()


def gelu_and_fetch(x, ct, kernel, mix):
    vmem = pl.BlockSpec(memory_space=pltpu.VMEM)
    return pl.pallas_call(
        gelu_kernel,
        out_shape=tuple(pltpu.VMEM(a.shape, jnp.bfloat16) for a in (x, ct, kernel, mix)),
        in_specs=[pl.BlockSpec(memory_space=pl.ANY)] * 4,
        out_specs=(vmem,) * 4,
        scratch_shapes=[pltpu.VMEM(x.shape, jnp.bfloat16), pltpu.SemaphoreType.DMA((4,))],
        compiler_params=pltpu.CompilerParams(vmem_limit_bytes=24 << 20),
        cost_estimate=pl.CostEstimate(
            flops=4 * 10**6, bytes_accessed=7 * 10**6, transcendentals=4 * 10**5
        ),
    )(*(pltpu.with_memory_space_constraint(a, pltpu.HBM) for a in (x, ct, kernel, mix)))


def pre_grad_kernel(act, ct, kernel, mix, preact, pre_grad):
    count = ct.shape[0]
    total = sum(
        jnp.dot(
            act[tap * DILATION_STEP : tap * DILATION_STEP + count],
            kernel[tap],
            preferred_element_type=jnp.float32,
        )
        for tap in range(3)
    )
    preact[...] = total
    grad_hidden = lax.dot_general(
        ct[...], mix[...], (((1,), (1,)), ((), ())), preferred_element_type=jnp.float32
    )
    pre_grad[...] = (grad_hidden * slope(preact[...])).astype(jnp.bfloat16)


def preact_and_grad(act, ct, kernel, mix):
    count, inner = ct.shape[0], mix.shape[0]
    vmem = pl.BlockSpec(memory_space=pltpu.VMEM)
    return pl.pallas_call(
        pre_grad_kernel,
        out_shape=(
            jax.ShapeDtypeStruct((count, inner), jnp.float32),
            jax.ShapeDtypeStruct((count, inner), jnp.bfloat16),
        ),
        in_specs=[vmem] * 4,
        out_specs=(vmem, vmem),
        compiler_params=pltpu.CompilerParams(vmem_limit_bytes=24 << 20),
        cost_estimate=pl.CostEstimate(
            flops=12 * 10**8, bytes_accessed=6 * 10**6, transcendentals=10**5
        ),
    )(act, ct, kernel, mix)


def gradient_kernel(
    core, act_a, act_b, grad_a, grad_b, select_all, ordered_far,
    whole, select, ordered, sem, out_sems,
):
    fetch = pltpu.make_async_copy(select_all.at[core[0]], select, sem)
    fetch.start()
    count, inner = grad_a.shape
    channels = act_a.shape[1]
    left_a, left_b = grad_a[...].T, grad_b[...].T
    width = 512
    for j in range(3 * channels // width):
        tap, ch = divmod(j * width, channels)
        rows = slice(tap * DILATION_STEP, tap * DILATION_STEP + count)
        part = jnp.dot(
            left_a, act_a[rows, ch : ch + width], preferred_element_type=jnp.float32
        ) + jnp.dot(left_b, act_b[rows, ch : ch + width], preferred_element_type=jnp.float32)
        whole[j * width : (j + 1) * width] = part.astype(jnp.bfloat16).T
    fetch.wait()
    piece, window = select.shape[1] // X, select.shape[2]
    block = 3 * channels // Y
    stores = []
    for y in range(Y):
        blocks = []
        for z in range(Z):
            start = y * block + z * 128
            blocks.append(
                lax.dot_general(
                    select[z],
                    whole[start : start + window],
                    (((1,), (0,)), ((), ())),
                    preferred_element_type=jnp.float32,
                )
            )
        for x in range(X):
            parts = []
            for four in range(0, Z, 4):
                a, b, c, d = (
                    held[x * piece : (x + 1) * piece] for held in blocks[four : four + 4]
                )
                parts += [a[:16], a[16:] + b[:8], b[8:16], b[16:] + c[:8]]
                parts += [c[8:16], c[16:] + d[:8], d[8:]]
            ordered[y * X + x] = jnp.concatenate(parts, 0).astype(jnp.bfloat16)
        span = slice(y * X, (y + 1) * X)
        stores.append(pltpu.make_async_copy(ordered.at[span], ordered_far.at[span], out_sems.at[y]))
        stores[-1].start()
    for store in stores:
        store.wait()


def y_x_terms(act_a, act_b, grad_a, grad_b):
    inner = grad_a.shape[1]
    rows = 3 * act_a.shape[1] // (Y * Z * CORES * X)
    select = jnp.asarray(owned_rows(rows))
    vmem = pl.BlockSpec(memory_space=pltpu.VMEM)
    ordered = pl.pallas_call(
        gradient_kernel,
        out_shape=pltpu.HBM((Y * X, Z * rows, inner), jnp.bfloat16),
        in_specs=[pl.BlockSpec(memory_space=pltpu.SMEM)]
        + [vmem] * 4
        + [pl.BlockSpec(memory_space=pl.ANY)],
        out_specs=pl.BlockSpec(memory_space=pl.ANY),
        scratch_shapes=[
            pltpu.VMEM((3 * act_a.shape[1], inner), jnp.bfloat16),
            pltpu.VMEM(select.shape[1:], jnp.bfloat16),
            pltpu.VMEM((Y * X, Z * rows, inner), jnp.bfloat16),
            pltpu.SemaphoreType.DMA,
            pltpu.SemaphoreType.DMA((Y,)),
        ],
        compiler_params=pltpu.CompilerParams(vmem_limit_bytes=24 << 20),
        cost_estimate=pl.CostEstimate(
            flops=3 * 10**9, bytes_accessed=6 * 10**6, transcendentals=0
        ),
    )(lax.axis_index("core").astype(jnp.int32)[None], act_a, act_b, grad_a, grad_b, pltpu.with_memory_space_constraint(select, pltpu.HBM))
    return lax.all_to_all(ordered, ("y", "x"), 0, 0, tiled=True)


def z_sum(terms):
    rows, inner = terms.shape[1] // Z, terms.shape[2]
    part = jnp.sum(terms.astype(jnp.float32), 0).astype(jnp.bfloat16)
    terms = lax.all_to_all(part.reshape(Z, rows, inner), "z", 0, 0, tiled=True)
    return jnp.sum(terms.astype(jnp.float32), 0).reshape(-1)


def body(inputs, cotangent, convolution_kernel, mix_weight):
    seqs, position_count, channels = inputs.shape
    x = inputs[0]
    ct = cotangent[0]
    step = DILATION_STEP
    core = lax.axis_index("core")
    last = position_count - step

    def padded(values, outer, inner):
        first = core == 0
        return jnp.concatenate(
            [jnp.where(first, outer, inner), values, jnp.where(first, inner, outer)], 0
        )

    outer = next_chip_edges(lax.dynamic_slice_in_dim(x, core * last, step, 0))
    inside = swap_cores(lax.dynamic_slice_in_dim(x, (1 - core) * last, step, 0))
    act, ct_near, kernel_near, mix_near = gelu_and_fetch(x, ct, convolution_kernel, mix_weight)
    activated = padded(act, gelu(outer), gelu(inside))
    activated = lax.optimization_barrier(activated)
    activated_pair = swap_cores(activated)
    preact, pre_grad = preact_and_grad(activated, ct_near, kernel_near, mix_near)
    pre_grad, activated_pair = lax.optimization_barrier((pre_grad, activated_pair))
    pre_grad_pair = swap_cores(pre_grad)
    terms = y_x_terms(activated, activated_pair, pre_grad, pre_grad_pair)

    outer = next_chip_edges(lax.dynamic_slice_in_dim(pre_grad, core * last, step, 0))
    inside = lax.dynamic_slice_in_dim(pre_grad_pair, core * last, step, 0)
    padded_grad = padded(pre_grad, outer, inside)
    hidden = gelu(preact)
    mixed = jnp.dot(hidden, mix_weight, preferred_element_type=jnp.float32)
    outputs = (x.astype(jnp.float32) + mixed).astype(jnp.bfloat16)
    act_grad = sum(
        lax.dot_general(
            padded_grad[(2 - k) * step : (2 - k) * step + position_count],
            convolution_kernel[k],
            (((1,), (1,)), ((), ())),
            preferred_element_type=jnp.float32,
        )
        for k in range(3)
    )
    grad_inputs = (
        ct.astype(jnp.float32) + act_grad * gelu_slope(x.astype(jnp.float32))
    ).astype(jnp.bfloat16)
    terms, grad_inputs = lax.optimization_barrier((terms, grad_inputs))
    factor = 1.0 / math.sqrt(seqs * position_count * Y * Z * CORES * X)
    grad_conv = z_sum(terms) * factor
    return outputs[None], grad_inputs[None], grad_conv


def solution(mesh):
    devices = mesh.devices.reshape(Y, Z, CORES, X)
    fine = Mesh(devices, ("y", "z", "core", "x"))
    rows = P("x", SEQ, None)
    return jax.shard_map(
        body,
        mesh=fine,
        in_specs=(rows, rows, P(), P()),
        out_specs=(rows, rows, P(("y", "z", "core", "x"))),
        check_vma=False,
    )
```

```python
import math

import jax
import jax.numpy as jnp
import numpy as np
from jax import lax
from jax.experimental import pallas as pl
from jax.experimental.pallas import tpu as pltpu
from jax.sharding import Mesh, PartitionSpec as P

DILATION_STEP = 16
Y, Z, CORES, X = 4, 8, 2, 4
SEQ = ("y", "z", "core")


def next_chip_edges(edge):
    pairs = [(2 * k + 1, 2 * k + 2) for k in range(Y * Z - 1)]
    return lax.ppermute(edge, SEQ, pairs + [(b, a) for a, b in pairs])


def swap_cores(values):
    return lax.ppermute(values, "core", [(0, 1), (1, 0)])


def gelu(values):
    return jax.nn.gelu(values.astype(jnp.float32)).astype(jnp.bfloat16)


def gelu_slope(values):
    return jax.vjp(jax.nn.gelu, values)[1](jnp.ones_like(values))[0]


def owned_rows(rows):
    piece = rows + 6
    held = np.zeros((CORES, Z, X * piece, 256), np.float32)
    for core in range(CORES):
        for z in range(Z):
            for x in range(X):
                for i in range(rows):
                    target = x * piece + rows * z % 8 + i
                    held[core, z, target, ((z * CORES + core) * X + x) * rows + i - 128 * z] = 1
    return held.astype(jnp.bfloat16)


def slope(values):
    root, cube = 0.7978845608, 0.044715
    square = values * values
    wave = jnp.tanh(root * values * (1.0 + cube * square))
    return 0.5 * (1.0 + wave) + 0.5 * values * (1.0 - wave * wave) * (
        root * (1.0 + 3.0 * cube * square)
    )


def gelu_kernel(x_far, ct_far, kernel_far, mix_far, act, ct, kernel, mix, x, sems):
    copies = [
        pltpu.make_async_copy(source, target, sems.at[i])
        for i, (source, target) in enumerate(
            ((x_far, x), (kernel_far, kernel), (mix_far, mix), (ct_far, ct))
        )
    ]
    for copy in copies:
        copy.start()
    copies[0].wait()
    act[...] = gelu(x[...])
    for copy in copies[1:]:
        copy.wait()


def gelu_and_fetch(x, ct, kernel, mix):
    vmem = pl.BlockSpec(memory_space=pltpu.VMEM)
    return pl.pallas_call(
        gelu_kernel,
        out_shape=tuple(pltpu.VMEM(a.shape, jnp.bfloat16) for a in (x, ct, kernel, mix)),
        in_specs=[pl.BlockSpec(memory_space=pl.ANY)] * 4,
        out_specs=(vmem,) * 4,
        scratch_shapes=[pltpu.VMEM(x.shape, jnp.bfloat16), pltpu.SemaphoreType.DMA((4,))],
        compiler_params=pltpu.CompilerParams(vmem_limit_bytes=24 << 20),
        cost_estimate=pl.CostEstimate(
            flops=4 * 10**6, bytes_accessed=7 * 10**6, transcendentals=4 * 10**5
        ),
    )(*(pltpu.with_memory_space_constraint(a, pltpu.HBM) for a in (x, ct, kernel, mix)))


def pre_grad_kernel(act, ct, kernel, mix, preact, pre_grad):
    count = ct.shape[0]
    total = sum(
        jnp.dot(
            act[tap * DILATION_STEP : tap * DILATION_STEP + count],
            kernel[tap],
            preferred_element_type=jnp.float32,
        )
        for tap in range(3)
    )
    preact[...] = total
    grad_hidden = lax.dot_general(
        ct[...], mix[...], (((1,), (1,)), ((), ())), preferred_element_type=jnp.float32
    )
    pre_grad[...] = (grad_hidden * slope(preact[...])).astype(jnp.bfloat16)


def preact_and_grad(act, ct, kernel, mix):
    count, inner = ct.shape[0], mix.shape[0]
    vmem = pl.BlockSpec(memory_space=pltpu.VMEM)
    return pl.pallas_call(
        pre_grad_kernel,
        out_shape=(
            jax.ShapeDtypeStruct((count, inner), jnp.float32),
            jax.ShapeDtypeStruct((count, inner), jnp.bfloat16),
        ),
        in_specs=[vmem] * 4,
        out_specs=(vmem, vmem),
        compiler_params=pltpu.CompilerParams(vmem_limit_bytes=24 << 20),
        cost_estimate=pl.CostEstimate(
            flops=12 * 10**8, bytes_accessed=6 * 10**6, transcendentals=10**5
        ),
    )(act, ct, kernel, mix)


def gradient_kernel(
    core, act_a, act_b, grad_a, grad_b, select_all, ordered_far,
    whole, select, ordered, sem, out_sems,
):
    fetch = pltpu.make_async_copy(select_all.at[core[0]], select, sem)
    fetch.start()
    count, inner = grad_a.shape
    channels = act_a.shape[1]
    left_a, left_b = grad_a[...].T, grad_b[...].T
    width = 512
    for j in range(3 * channels // width):
        tap, ch = divmod(j * width, channels)
        rows = slice(tap * DILATION_STEP, tap * DILATION_STEP + count)
        part = jnp.dot(
            left_a, act_a[rows, ch : ch + width], preferred_element_type=jnp.float32
        ) + jnp.dot(left_b, act_b[rows, ch : ch + width], preferred_element_type=jnp.float32)
        whole[j * width : (j + 1) * width] = part.astype(jnp.bfloat16).T
    fetch.wait()
    piece, window = select.shape[1] // X, select.shape[2]
    block = 3 * channels // Y
    stores = []
    for y in range(Y):
        blocks = []
        for z in range(Z):
            start = y * block + z * 128
            blocks.append(
                lax.dot_general(
                    select[z],
                    whole[start : start + window],
                    (((1,), (0,)), ((), ())),
                    preferred_element_type=jnp.float32,
                )
            )
        for x in range(X):
            parts = []
            for four in range(0, Z, 4):
                a, b, c, d = (
                    held[x * piece : (x + 1) * piece] for held in blocks[four : four + 4]
                )
                parts += [a[:16], a[16:] + b[:8], b[8:16], b[16:] + c[:8]]
                parts += [c[8:16], c[16:] + d[:8], d[8:]]
            ordered[y * X + x] = jnp.concatenate(parts, 0).astype(jnp.bfloat16)
        span = slice(y * X, (y + 1) * X)
        stores.append(pltpu.make_async_copy(ordered.at[span], ordered_far.at[span], out_sems.at[y]))
        stores[-1].start()
    for store in stores:
        store.wait()


def y_x_terms(act_a, act_b, grad_a, grad_b):
    inner = grad_a.shape[1]
    rows = 3 * act_a.shape[1] // (Y * Z * CORES * X)
    select = jnp.asarray(owned_rows(rows))
    vmem = pl.BlockSpec(memory_space=pltpu.VMEM)
    ordered = pl.pallas_call(
        gradient_kernel,
        out_shape=pltpu.HBM((Y * X, Z * rows, inner), jnp.bfloat16),
        in_specs=[pl.BlockSpec(memory_space=pltpu.SMEM)]
        + [vmem] * 4
        + [pl.BlockSpec(memory_space=pl.ANY)],
        out_specs=pl.BlockSpec(memory_space=pl.ANY),
        scratch_shapes=[
            pltpu.VMEM((3 * act_a.shape[1], inner), jnp.bfloat16),
            pltpu.VMEM(select.shape[1:], jnp.bfloat16),
            pltpu.VMEM((Y * X, Z * rows, inner), jnp.bfloat16),
            pltpu.SemaphoreType.DMA,
            pltpu.SemaphoreType.DMA((Y,)),
        ],
        compiler_params=pltpu.CompilerParams(vmem_limit_bytes=24 << 20),
        cost_estimate=pl.CostEstimate(
            flops=3 * 10**9, bytes_accessed=6 * 10**6, transcendentals=0
        ),
    )(lax.axis_index("core").astype(jnp.int32)[None], act_a, act_b, grad_a, grad_b, pltpu.with_memory_space_constraint(select, pltpu.HBM))
    return lax.all_to_all(ordered, ("y", "x"), 0, 0, tiled=True)


def z_sum(terms):
    rows, inner = terms.shape[1] // Z, terms.shape[2]
    part = jnp.sum(terms.astype(jnp.float32), 0).astype(jnp.bfloat16)
    terms = lax.all_to_all(part.reshape(Z, rows, inner), "z", 0, 0, tiled=True)
    return jnp.sum(terms.astype(jnp.float32), 0).reshape(-1)


def body(inputs, cotangent, convolution_kernel, mix_weight):
    seqs, position_count, channels = inputs.shape
    x = inputs[0]
    ct = cotangent[0]
    step = DILATION_STEP
    core = lax.axis_index("core")
    last = position_count - step

    def padded(values, outer, inner):
        first = core == 0
        return jnp.concatenate(
            [jnp.where(first, outer, inner), values, jnp.where(first, inner, outer)], 0
        )

    outer = next_chip_edges(lax.dynamic_slice_in_dim(x, core * last, step, 0))
    inside = swap_cores(lax.dynamic_slice_in_dim(x, (1 - core) * last, step, 0))
    act, ct_near, kernel_near, mix_near = gelu_and_fetch(x, ct, convolution_kernel, mix_weight)
    activated = padded(act, gelu(outer), gelu(inside))
    activated = lax.optimization_barrier(activated)
    activated_pair = swap_cores(activated)
    preact, pre_grad = preact_and_grad(activated, ct_near, kernel_near, mix_near)
    pre_grad, activated_pair = lax.optimization_barrier((pre_grad, activated_pair))
    pre_grad_pair = swap_cores(pre_grad)
    terms = y_x_terms(activated, activated_pair, pre_grad, pre_grad_pair)

    outer = next_chip_edges(lax.dynamic_slice_in_dim(pre_grad, core * last, step, 0))
    inside = lax.dynamic_slice_in_dim(pre_grad_pair, core * last, step, 0)
    padded_grad = padded(pre_grad, outer, inside)
    hidden = gelu(preact)
    mixed = jnp.dot(hidden, mix_weight, preferred_element_type=jnp.float32)
    outputs = (x.astype(jnp.float32) + mixed).astype(jnp.bfloat16)
    act_grad = sum(
        lax.dot_general(
            padded_grad[(2 - k) * step : (2 - k) * step + position_count],
            convolution_kernel[k],
            (((1,), (1,)), ((), ())),
            preferred_element_type=jnp.float32,
        )
        for k in range(3)
    )
    grad_inputs = (
        ct.astype(jnp.float32) + act_grad * gelu_slope(x.astype(jnp.float32))
    ).astype(jnp.bfloat16)
    terms, grad_inputs, outputs = lax.optimization_barrier((terms, grad_inputs, outputs))
    factor = 1.0 / math.sqrt(seqs * position_count * Y * Z * CORES * X)
    grad_conv = z_sum(terms) * factor
    return outputs[None], grad_inputs[None], grad_conv


def solution(mesh):
    devices = mesh.devices.reshape(Y, Z, CORES, X)
    fine = Mesh(devices, ("y", "z", "core", "x"))
    rows = P("x", SEQ, None)
    return jax.shard_map(
        body,
        mesh=fine,
        in_specs=(rows, rows, P(), P()),
        out_specs=(rows, rows, P(("y", "z", "core", "x"))),
        check_vma=False,
    )
```

```python
import math

import jax
import jax.numpy as jnp
import numpy as np
from jax import lax
from jax.experimental import pallas as pl
from jax.experimental.pallas import tpu as pltpu
from jax.sharding import Mesh, PartitionSpec as P

DILATION_STEP = 16
Y, Z, CORES, X = 4, 8, 2, 4
SEQ = ("y", "z", "core")


def next_chip_edges(edge):
    pairs = [(2 * k + 1, 2 * k + 2) for k in range(Y * Z - 1)]
    return lax.ppermute(edge, SEQ, pairs + [(b, a) for a, b in pairs])


def swap_cores(values):
    return lax.ppermute(values, "core", [(0, 1), (1, 0)])


def gelu(values):
    return jax.nn.gelu(values.astype(jnp.float32)).astype(jnp.bfloat16)


def gelu_slope(values):
    return jax.vjp(jax.nn.gelu, values)[1](jnp.ones_like(values))[0]


def owned_rows(rows):
    piece = rows + 6
    held = np.zeros((CORES, Z, X * piece, 256), np.float32)
    for core in range(CORES):
        for z in range(Z):
            for x in range(X):
                for i in range(rows):
                    target = x * piece + rows * z % 8 + i
                    held[core, z, target, ((z * CORES + core) * X + x) * rows + i - 128 * z] = 1
    return held.astype(jnp.bfloat16)


def slope(values):
    root, cube = 0.7978845608, 0.044715
    square = values * values
    wave = jnp.tanh(root * values * (1.0 + cube * square))
    return 0.5 * (1.0 + wave) + 0.5 * values * (1.0 - wave * wave) * (
        root * (1.0 + 3.0 * cube * square)
    )


def gelu_kernel(x_far, ct_far, kernel_far, mix_far, act, ct, kernel, mix, x, sems):
    copies = [
        pltpu.make_async_copy(source, target, sems.at[i])
        for i, (source, target) in enumerate(
            ((x_far, x), (kernel_far, kernel), (mix_far, mix), (ct_far, ct))
        )
    ]
    for copy in copies:
        copy.start()
    copies[0].wait()
    act[...] = gelu(x[...])
    for copy in copies[1:]:
        copy.wait()


def gelu_and_fetch(x, ct, kernel, mix):
    vmem = pl.BlockSpec(memory_space=pltpu.VMEM)
    return pl.pallas_call(
        gelu_kernel,
        out_shape=tuple(pltpu.VMEM(a.shape, jnp.bfloat16) for a in (x, ct, kernel, mix)),
        in_specs=[pl.BlockSpec(memory_space=pl.ANY)] * 4,
        out_specs=(vmem,) * 4,
        scratch_shapes=[pltpu.VMEM(x.shape, jnp.bfloat16), pltpu.SemaphoreType.DMA((4,))],
        compiler_params=pltpu.CompilerParams(vmem_limit_bytes=24 << 20),
        cost_estimate=pl.CostEstimate(
            flops=4 * 10**6, bytes_accessed=7 * 10**6, transcendentals=4 * 10**5
        ),
    )(*(pltpu.with_memory_space_constraint(a, pltpu.HBM) for a in (x, ct, kernel, mix)))


def pre_grad_kernel(act, ct, kernel, mix, preact, pre_grad):
    count = ct.shape[0]
    total = sum(
        jnp.dot(
            act[tap * DILATION_STEP : tap * DILATION_STEP + count],
            kernel[tap],
            preferred_element_type=jnp.float32,
        )
        for tap in range(3)
    )
    preact[...] = total
    grad_hidden = lax.dot_general(
        ct[...], mix[...], (((1,), (1,)), ((), ())), preferred_element_type=jnp.float32
    )
    pre_grad[...] = (grad_hidden * slope(preact[...])).astype(jnp.bfloat16)


def preact_and_grad(act, ct, kernel, mix):
    count, inner = ct.shape[0], mix.shape[0]
    vmem = pl.BlockSpec(memory_space=pltpu.VMEM)
    return pl.pallas_call(
        pre_grad_kernel,
        out_shape=(
            jax.ShapeDtypeStruct((count, inner), jnp.float32),
            jax.ShapeDtypeStruct((count, inner), jnp.bfloat16),
        ),
        in_specs=[vmem] * 4,
        out_specs=(vmem, vmem),
        compiler_params=pltpu.CompilerParams(vmem_limit_bytes=24 << 20),
        cost_estimate=pl.CostEstimate(
            flops=12 * 10**8, bytes_accessed=6 * 10**6, transcendentals=10**5
        ),
    )(act, ct, kernel, mix)


def gradient_kernel(
    core, act_a, act_b, grad_a, grad_b, select_all, ordered_far,
    whole, select, ordered, sem, out_sems,
):
    fetch = pltpu.make_async_copy(select_all.at[core[0]], select, sem)
    fetch.start()
    count, inner = grad_a.shape
    channels = act_a.shape[1]
    left_a, left_b = grad_a[...].T, grad_b[...].T
    width = 512
    for j in range(3 * channels // width):
        tap, ch = divmod(j * width, channels)
        rows = slice(tap * DILATION_STEP, tap * DILATION_STEP + count)
        part = jnp.dot(
            left_a, act_a[rows, ch : ch + width], preferred_element_type=jnp.float32
        ) + jnp.dot(left_b, act_b[rows, ch : ch + width], preferred_element_type=jnp.float32)
        whole[j * width : (j + 1) * width] = part.astype(jnp.bfloat16).T
    fetch.wait()
    piece, window = select.shape[1] // X, select.shape[2]
    block = 3 * channels // Y
    stores = []
    for y in range(Y):
        blocks = []
        for z in range(Z):
            start = y * block + z * 128
            blocks.append(
                lax.dot_general(
                    select[z],
                    whole[start : start + window],
                    (((1,), (0,)), ((), ())),
                    preferred_element_type=jnp.float32,
                )
            )
        for x in range(X):
            parts = []
            for four in range(0, Z, 4):
                a, b, c, d = (
                    held[x * piece : (x + 1) * piece] for held in blocks[four : four + 4]
                )
                parts += [a[:16], a[16:] + b[:8], b[8:16], b[16:] + c[:8]]
                parts += [c[8:16], c[16:] + d[:8], d[8:]]
            at = x * Y + y
            ordered[at] = jnp.concatenate(parts, 0).astype(jnp.bfloat16)
            stores.append(pltpu.make_async_copy(ordered.at[at], ordered_far.at[at], out_sems.at[at]))
            stores[-1].start()
    for store in stores:
        store.wait()


def y_x_terms(act_a, act_b, grad_a, grad_b):
    inner = grad_a.shape[1]
    rows = 3 * act_a.shape[1] // (Y * Z * CORES * X)
    select = jnp.asarray(owned_rows(rows))
    vmem = pl.BlockSpec(memory_space=pltpu.VMEM)
    ordered = pl.pallas_call(
        gradient_kernel,
        out_shape=pltpu.HBM((Y * X, Z * rows, inner), jnp.bfloat16),
        in_specs=[pl.BlockSpec(memory_space=pltpu.SMEM)]
        + [vmem] * 4
        + [pl.BlockSpec(memory_space=pl.ANY)],
        out_specs=pl.BlockSpec(memory_space=pl.ANY),
        scratch_shapes=[
            pltpu.VMEM((3 * act_a.shape[1], inner), jnp.bfloat16),
            pltpu.VMEM(select.shape[1:], jnp.bfloat16),
            pltpu.VMEM((Y * X, Z * rows, inner), jnp.bfloat16),
            pltpu.SemaphoreType.DMA,
            pltpu.SemaphoreType.DMA((Y * X,)),
        ],
        compiler_params=pltpu.CompilerParams(vmem_limit_bytes=24 << 20),
        cost_estimate=pl.CostEstimate(
            flops=3 * 10**9, bytes_accessed=6 * 10**6, transcendentals=0
        ),
    )(lax.axis_index("core").astype(jnp.int32)[None], act_a, act_b, grad_a, grad_b, pltpu.with_memory_space_constraint(select, pltpu.HBM))
    return lax.all_to_all(ordered, ("x", "y"), 0, 0, tiled=True)


def z_sum(terms):
    rows, inner = terms.shape[1] // Z, terms.shape[2]
    part = jnp.sum(terms.astype(jnp.float32), 0).astype(jnp.bfloat16)
    terms = lax.all_to_all(part.reshape(Z, rows, inner), "z", 0, 0, tiled=True)
    return jnp.sum(terms.astype(jnp.float32), 0).reshape(-1)


def body(inputs, cotangent, convolution_kernel, mix_weight):
    seqs, position_count, channels = inputs.shape
    x = inputs[0]
    ct = cotangent[0]
    step = DILATION_STEP
    core = lax.axis_index("core")
    last = position_count - step

    def padded(values, outer, inner):
        first = core == 0
        return jnp.concatenate(
            [jnp.where(first, outer, inner), values, jnp.where(first, inner, outer)], 0
        )

    outer = next_chip_edges(lax.dynamic_slice_in_dim(x, core * last, step, 0))
    inside = swap_cores(lax.dynamic_slice_in_dim(x, (1 - core) * last, step, 0))
    act, ct_near, kernel_near, mix_near = gelu_and_fetch(x, ct, convolution_kernel, mix_weight)
    activated = padded(act, gelu(outer), gelu(inside))
    activated = lax.optimization_barrier(activated)
    activated_pair = swap_cores(activated)
    preact, pre_grad = preact_and_grad(activated, ct_near, kernel_near, mix_near)
    pre_grad, activated_pair = lax.optimization_barrier((pre_grad, activated_pair))
    pre_grad_pair = swap_cores(pre_grad)
    terms = y_x_terms(activated, activated_pair, pre_grad, pre_grad_pair)

    outer = next_chip_edges(lax.dynamic_slice_in_dim(pre_grad, core * last, step, 0))
    inside = lax.dynamic_slice_in_dim(pre_grad_pair, core * last, step, 0)
    padded_grad = padded(pre_grad, outer, inside)
    hidden = gelu(preact)
    mixed = jnp.dot(hidden, mix_weight, preferred_element_type=jnp.float32)
    outputs = (x.astype(jnp.float32) + mixed).astype(jnp.bfloat16)
    act_grad = sum(
        lax.dot_general(
            padded_grad[(2 - k) * step : (2 - k) * step + position_count],
            convolution_kernel[k],
            (((1,), (1,)), ((), ())),
            preferred_element_type=jnp.float32,
        )
        for k in range(3)
    )
    grad_inputs = (
        ct.astype(jnp.float32) + act_grad * gelu_slope(x.astype(jnp.float32))
    ).astype(jnp.bfloat16)
    terms, grad_inputs, outputs = lax.optimization_barrier((terms, grad_inputs, outputs))
    factor = 1.0 / math.sqrt(seqs * position_count * Y * Z * CORES * X)
    grad_conv = z_sum(terms) * factor
    return outputs[None], grad_inputs[None], grad_conv


def solution(mesh):
    devices = mesh.devices.reshape(Y, Z, CORES, X)
    fine = Mesh(devices, ("y", "z", "core", "x"))
    rows = P("x", SEQ, None)
    return jax.shard_map(
        body,
        mesh=fine,
        in_specs=(rows, rows, P(), P()),
        out_specs=(rows, rows, P(("y", "z", "core", "x"))),
        check_vma=False,
    )
```
